32 devices in a mesh: col: 8 (over z, x), row: 4 (over y, core).
Axes of the slice: x: 2, y: 2, z: 4, core: 2. Of those that a mesh axis runs over, the one named last changes fastest.
Arguments:
- position: float32 [128, 16384], P(None, ('col', 'row')), may hold values from -6 to 6
- momentum: float32 [128, 16384], P(None, ('col', 'row')), may hold values from -6 to 6
- row_factors: bfloat16 [16384, 16, 128], P(('col', 'row')), may hold values from -1 to 1
- col_factors: bfloat16 [16384, 16, 128], P(('col', 'row')), may hold values from -1 to 1
- tile_ranks: int32 [16, 16], replicated, may hold values from 16 to 128, as said below
- log_mean: float32 [16384], P(('col', 'row')), may hold values from -0.5 to 0.5
- counts: int32 [16384], P(('col', 'row')), may hold values from 0 to 11
- step_size: float32 [128], replicated, may hold values from 0.1 to 0.3
Outputs:
- new_position: float32 [128, 16384], P(None, ('col', 'row'))
- new_momentum: float32 [128, 16384], P(None, ('col', 'row'))
- energy_change: float32 [128], replicated
The draws below stay inside these ranges and needn't reach their ends.
Inputs may be any that keep to these rules, and one draw needn't show every extreme that they name: `tile_ranks`: every entry is a multiple of 16; in every draw some tile has rank 16 and some tile has rank 128.
All inputs are finite; a program needn't handle non-finite values.
Results may differ from the reference program's by a relative error of at most 0.004.
Values may be sent and summed in bfloat16 or wider, within the bound.
A program may use at most 128 MiB of HBM per device.

```python
import math
import jax
import jax.numpy as jnp
from jax import lax

TILE_CELLS = 1024
RANK_MAX = 128
RANK_BLOCK = 16
CHAINS = 128
TILES = 16
CELLS = 16384


def draw_tile_ranks(key, part):
    total = TILES * TILES
    level_count = RANK_MAX // RANK_BLOCK
    level_key = jax.random.fold_in(key, 11)
    low_key = jax.random.fold_in(key, 12)
    high_key = jax.random.fold_in(key, 13)
    drawn = jax.random.randint(level_key, (total,), 1, level_count + 1)
    low_at = jax.random.randint(low_key, (), 0, total)
    high_at = (low_at + 1 + jax.random.randint(high_key, (), 0, total - 1)) % total
    drawn = drawn.at[low_at].set(1).at[high_at].set(level_count)
    return (drawn * RANK_BLOCK).reshape(TILES, TILES).astype(jnp.int32)


def draw_counts(key, part):
    cell_index = jnp.arange(CELLS, dtype=jnp.int32)
    ceiling = 3 + 9 * cell_index // CELLS
    drawn = jax.random.randint(jax.random.fold_in(key, 21), (CELLS,), 0, 1 << 20)
    return (drawn % (ceiling + 1)).astype(jnp.int32)


def unit_entries(key, shape):
    values = jnp.clip(jax.random.normal(key, shape, jnp.float32), -6.0, 6.0)
    return values


def draw_position(key, part):
    return unit_entries(jax.random.fold_in(key, 31), (CHAINS, CELLS))


def draw_row_factors(key, part):
    values = unit_entries(jax.random.fold_in(key, 41), (CELLS, TILES, RANK_MAX))
    scale = (TILES * RANK_MAX) ** (-0.5)
    return (values * scale).astype(jnp.bfloat16)


def draw_col_factors(key, part):
    values = unit_entries(jax.random.fold_in(key, 51), (CELLS, TILES, RANK_MAX))
    scale = TILE_CELLS ** (-0.5)
    return (values * scale).astype(jnp.bfloat16)


def steps_of(own_key, dims, shards, low, largest):
    level, own = 1.0, jax.random.fold_in(own_key, 6)
    for axis_at, shards_of in shards:
        draws = jnp.exp(jax.random.uniform(jax.random.fold_in(own, axis_at), (shards_of,), jnp.float32, low / len(shards), largest / len(shards)))
        level = level * jnp.repeat(draws, dims[axis_at] // shards_of).reshape([-1 if axis == axis_at else 1 for axis in range(len(dims))])
    return level


def scatter_about(key, dims, scale, most, split=(), kind=jnp.bfloat16):
    level = steps_of(key, dims, split, -0.22, 0.18) if split else 1.0
    array = jax.random.normal(key, dims, jnp.float32) * scale * level
    return jnp.minimum(jnp.maximum(array, -most), most).astype(kind)


def setup_inputs(seed: int = 0) -> dict:
    key_list = jax.random.split(jax.random.key(seed), 9)
    return {
        "position": draw_position(jax.random.fold_in(key_list[8], 71), 0),
        "momentum": scatter_about(key_list[1], (CHAINS, CELLS), 1.0, 6.0, ((1, 32),), jnp.float32),
        "row_factors": draw_row_factors(jax.random.fold_in(key_list[8], 71), 0),
        "col_factors": draw_col_factors(jax.random.fold_in(key_list[8], 71), 0),
        "tile_ranks": draw_tile_ranks(jax.random.fold_in(key_list[8], 71), 0),
        "log_mean": jnp.clip(jax.random.uniform(key_list[5], (CELLS,), jnp.float32, -0.5, 0.5) * steps_of(key_list[5], (CELLS,), ((0, 32),), -0.4, 0.0), -0.5, 0.5),
        "counts": draw_counts(jax.random.fold_in(key_list[8], 71), 0),
        "step_size": jnp.clip(jnp.exp(jax.random.uniform(key_list[7], (CHAINS,), jnp.float32, math.log(0.1), math.log(0.3))), 0.1, 0.3),
    }


def half_round(values):
    return lax.optimization_barrier(values.astype(jnp.bfloat16)).astype(jnp.float32)


def gradient(position, row_factors, col_factors, alive_mask, log_mean, counts):
    chains = position.shape[0]
    half_cells = TILE_CELLS // 2
    cell_grid = half_round(position).reshape(chains, TILES, 2, half_cells)
    col_grid = col_factors.reshape(TILES, 2, half_cells, TILES, RANK_MAX)
    row_grid = row_factors.reshape(TILES, 2, half_cells, TILES, RANK_MAX)
    tile_order = jnp.arange(TILES, dtype=jnp.int32)

    def forward(column):
        factor_block = col_grid[column].astype(jnp.float32)
        values = cell_grid[:, column]
        partial_value = jnp.einsum('syik,hsy->sikh', factor_block, values)
        partial_value = half_round(partial_value * alive_mask[:, column][None, :, :, None])
        return half_round(partial_value[0] + partial_value[1])

    coefficients = lax.map(forward, tile_order)

    def field_rows(tile_index):
        factor_block = row_grid[tile_index].astype(jnp.float32)
        coefficient = coefficients[:, tile_index]
        return jnp.einsum('sxjk,jkh->hsx', factor_block, coefficient)

    latent_field = lax.map(field_rows, tile_order)
    latent_field = jnp.transpose(latent_field, (1, 0, 2, 3)).reshape(chains, CELLS)
    exponent = log_mean[None, :] + latent_field
    intensity = jnp.exp(exponent)
    rate_base = counts.astype(jnp.float32)[None, :]
    residual = rate_base - intensity
    residual_grid = half_round(residual).reshape(chains, TILES, 2, half_cells)

    def backward(tile_index):
        factor_block = row_grid[tile_index].astype(jnp.float32)
        values = residual_grid[:, tile_index]
        partial_value = jnp.einsum('sxjk,hsx->sjkh', factor_block, values)
        partial_value = half_round(partial_value * alive_mask[tile_index][None, :, :, None])
        return half_round(partial_value[0] + partial_value[1])

    returned = lax.map(backward, tile_order)

    def pull_columns(column):
        factor_block = col_grid[column].astype(jnp.float32)
        coefficient = returned[:, column]
        return jnp.einsum('syik,ikh->hsy', factor_block, coefficient)

    pulled = lax.map(pull_columns, tile_order)
    pulled = jnp.transpose(pulled, (1, 0, 2, 3)).reshape(chains, CELLS)
    pieces = intensity - rate_base * exponent + 0.5 * position * position
    return position - pulled, pieces


def reference(position, momentum, row_factors, col_factors, tile_ranks, log_mean, counts, step_size):
    levels = jnp.arange(RANK_MAX, dtype=jnp.int32)
    alive_mask = (levels[None, None, :] < tile_ranks[:, :, None]).astype(jnp.float32)
    half_step = 0.5 * step_size[:, None]
    full_step = step_size[:, None]
    forces, start_energy = gradient(position, row_factors, col_factors, alive_mask, log_mean, counts)
    moment = momentum - half_step * forces
    shifted = position + full_step * moment
    forces, unused = gradient(shifted, row_factors, col_factors, alive_mask, log_mean, counts)
    moment = moment - full_step * forces
    shifted = shifted + full_step * moment
    forces, end_energy = gradient(shifted, row_factors, col_factors, alive_mask, log_mean, counts)
    moment = moment - half_step * forces
    change = jnp.sum(end_energy - start_energy + 0.5 * (moment * moment - momentum * momentum), axis=1)
    return shifted, moment, change
```

```python
import functools

import jax
import jax.numpy as jnp
from jax import lax
from jax.experimental import pallas as pl
from jax.experimental.pallas import tpu as pltpu
from jax.sharding import PartitionSpec as P

MESH = pl.DeviceIdType.MESH
GROUPS = 2
SWAP = jnp.bfloat16
FULL = jnp.float32
HALF = jnp.bfloat16
FORWARD, BACKWARD = 0, 1


def kernel(
    row_size,
    pos, mom, col2, row2, log_mean, counts, step,
    new_pos, new_mom, energy,
    zs, ps, col_far, row_far, lm_far, cnt_far,
    out_buf, in_buf, swap_out, swap_in, gain,
    e_own, e_far, e_chip, e_all, e_part, e_rest,
    init_send, init_recv, send, recv, swap_send, swap_recv,
    tail_send, tail_recv, all_send, all_recv,
):
    halves = in_buf.shape[2]
    chains, cells = pos.shape
    ranked = in_buf.shape[4]
    block = chains // GROUPS

    me = lax.axis_index("col") * row_size + lax.axis_index("row")
    tile = me // 2
    core = me % 2
    side = tile % 2
    slot = tile // 2

    def address(index):
        return (index // row_size, index % row_size)

    partner = address(2 * tile + 1 - core)

    def peer(m):
        return address(2 * (2 * m + core) + side)

    def each_peer(action, at_home=None):
        def body(n, carry):
            action((slot + 1 + n) % halves)
            return carry

        lax.fori_loop(0, halves - 1, body, 0)

        @pl.when(core != side)
        def _():
            action(slot)

        if at_home is not None:
            @pl.when(core == side)
            def _():
                at_home()

    barrier = pltpu.get_barrier_semaphore()

    def greet(m):
        pl.semaphore_signal(barrier, inc=1, device_id=peer(m), device_id_type=MESH)

    each_peer(greet)
    pl.semaphore_signal(barrier, inc=1, device_id=partner, device_id_type=MESH)
    pl.semaphore_wait(barrier, halves + jnp.where(core == side, 0, 1))

    def remote(src, dst, s, r, where):
        return pltpu.make_async_remote_copy(
            src_ref=src, dst_ref=dst, send_sem=s, recv_sem=r,
            device_id=where, device_id_type=MESH,
        )

    first = [
        remote(src, dst, init_send.at[n], init_recv.at[n], partner)
        for n, (src, dst) in enumerate([
            (pos, zs.at[1]), (col2.at[1 - core], col_far),
            (log_mean, lm_far), (counts, cnt_far),
            (row2.at[1 - core], row_far), (mom, ps.at[1]),
        ])
    ]
    for copy in first:
        copy.start()
    zs[0] = pos[...]
    ps[0] = mom[...]
    gain[...] = jnp.zeros_like(gain)

    def rows(g):
        return pl.ds(g * block, block)

    def project(way, g, near, far, near_ref, far_ref):
        result = jnp.dot(near, near_ref[core], preferred_element_type=FULL)
        result += jnp.dot(far, far_ref[...], preferred_element_type=FULL)
        result = result.astype(HALF)
        for m in range(halves):
            out_buf[way, g, m] = result[:, m * ranked:(m + 1) * ranked]

        def start(m):
            remote(
                out_buf.at[way, g, m], in_buf.at[way, g, slot],
                send.at[way, g, m], recv.at[way, g, slot], peer(m),
            ).start()

        def keep():
            in_buf[way, g, slot] = out_buf[way, g, slot]

        each_peer(start, keep)

    def expand(way, g, near_ref, far_ref):
        def finish(m):
            copy = remote(
                out_buf.at[way, g, m], in_buf.at[way, g, m],
                send.at[way, g, m], recv.at[way, g, m], peer(m),
            )
            copy.wait_recv()
            copy.wait_send()

        each_peer(finish)
        held = jnp.concatenate([in_buf[way, g, m] for m in range(halves)], axis=1)
        dims = (((1,), (1,)), ((), ()))
        copies = []
        far = lax.dot_general(held, far_ref[...], dims, preferred_element_type=FULL)
        swap_out[way, g, 1] = far.astype(SWAP)
        copies.append(remote(
            swap_out.at[way, g, 1], swap_in.at[way, g, 0],
            swap_send.at[way, g, 0], swap_recv.at[way, g, 0], partner,
        ))
        copies[0].start()
        near = lax.dot_general(held, near_ref[core], dims, preferred_element_type=FULL)
        swap_out[way, g, 0] = near.astype(SWAP)
        copies.append(remote(
            swap_out.at[way, g, 0], swap_in.at[way, g, 1],
            swap_send.at[way, g, 1], swap_recv.at[way, g, 1], partner,
        ))
        copies[1].start()
        for copy in copies:
            copy.wait()
        near = near + swap_in[way, g, 0].astype(FULL)
        far = far + swap_in[way, g, 1].astype(FULL)
        return near, far

    def send_forward(g):
        project(
            FORWARD, g,
            zs[0, rows(g)].astype(HALF), zs[1, rows(g)].astype(HALF),
            col2, col_far,
        )

    first[0].wait()
    first[1].wait()
    for g in range(GROUPS):
        send_forward(g)
    for copy in first[2:]:
        copy.wait()

    def section(at, carry):
        sign = (at // 2 - (2 - at) // 2).astype(FULL)
        weight = jnp.where(at == 1, 1.0, 0.5).astype(FULL)
        for g in range(GROUPS):
            near, far = expand(FORWARD, g, row2, row_far)
            exponent = log_mean[...] + near
            intensity = jnp.exp(exponent)
            rate = counts[...].astype(FULL)
            residual = (rate - intensity).astype(HALF)
            residual_far = (
                cnt_far[...].astype(FULL) - jnp.exp(lm_far[...] + far)
            ).astype(HALF)
            project(BACKWARD, g, residual, residual_far, row2, row_far)
            values = zs[0, rows(g)]
            gain[rows(g)] += sign * (
                intensity - rate * exponent + 0.5 * values * values
            )
        for g in range(GROUPS):
            pulled = expand(BACKWARD, g, col2, col_far)
            size = step[rows(g)]
            for part in range(2):
                values = zs[part, rows(g)]
                moment = ps[part, rows(g)] - weight * size * (values - pulled[part])
                ps[part, rows(g)] = moment

                @pl.when(at < 2)
                def _():
                    zs[part, rows(g)] = values + size * moment

            @pl.when(at < 2)
            def _():
                send_forward(g)

        return carry

    lax.fori_loop(0, 3, section, 0)

    after = ps[0]
    before = mom[...]
    change = gain[...] + 0.5 * (after * after - before * before)
    lanes = e_own.shape[1]
    change = sum(change[:, n * lanes:(n + 1) * lanes] for n in range(cells // lanes))
    total = jnp.sum(change.T, axis=0, keepdims=True)
    e_own[...] = jnp.broadcast_to(total, e_own.shape)
    copy = remote(e_own, e_far, tail_send.at[0], tail_recv.at[0], partner)
    copy.start()
    new_pos[...] = zs[0]
    new_mom[...] = after
    copy.wait()
    e_chip[...] = e_own[...] + e_far[...]

    def spread(m):
        remote(
            e_chip, e_all.at[slot], all_send.at[m], all_recv.at[slot], peer(m)
        ).start()

    def spread_home():
        e_all[slot] = e_chip[...]

    def gather(m):
        copy = remote(e_chip, e_all.at[m], all_send.at[m], all_recv.at[m], peer(m))
        copy.wait_recv()
        copy.wait_send()

    each_peer(spread, spread_home)
    each_peer(gather)
    e_part[...] = jnp.sum(e_all[...], axis=0)
    copy = remote(e_part, e_rest, tail_send.at[1], tail_recv.at[1], partner)
    copy.start()
    copy.wait()
    energy[...] = e_part[...] + e_rest[...]


def on_device(
    row_size,
    position, momentum, row_factors, col_factors, tile_ranks, log_mean, counts, step_size
):
    chains, cells = position.shape
    tiles = tile_ranks.shape[0]
    halves = tiles // 2
    ranked = row_factors.shape[2]
    device = lax.axis_index(("col", "row"))
    tile = device // 2
    levels = jnp.arange(ranked, dtype=jnp.int32)
    col_ranks = lax.dynamic_slice_in_dim(tile_ranks, tile, 1, 1)[:, 0]
    row_ranks = lax.dynamic_slice_in_dim(tile_ranks, tile, 1, 0)[0]

    def prepare(factors, ranks):
        live = levels[None, :] < ranks[:, None]
        kept = jnp.where(live[None], factors, jnp.zeros_like(factors))
        kept = kept.reshape(cells, halves, 2, ranked)
        return jnp.transpose(kept, (2, 0, 1, 3)).reshape(2, cells, halves * ranked)

    block = chains // GROUPS
    vmem = pl.BlockSpec(memory_space=pltpu.VMEM)
    dma = pltpu.SemaphoreType.DMA
    small = pltpu.VMEM((8, chains), FULL)
    new_pos, new_mom, energy = pl.pallas_call(
        functools.partial(kernel, row_size),
        out_shape=(
            jax.ShapeDtypeStruct(position.shape, FULL),
            jax.ShapeDtypeStruct(position.shape, FULL),
            jax.ShapeDtypeStruct((8, chains), FULL),
        ),
        in_specs=[vmem] * 7,
        out_specs=(vmem, vmem, vmem),
        scratch_shapes=[
            pltpu.VMEM((2, chains, cells), FULL),
            pltpu.VMEM((2, chains, cells), FULL),
            pltpu.VMEM((cells, halves * ranked), HALF),
            pltpu.VMEM((cells, halves * ranked), HALF),
            pltpu.VMEM((1, cells), FULL),
            pltpu.VMEM((1, cells), jnp.int32),
            pltpu.VMEM((2, GROUPS, halves, block, ranked), HALF),
            pltpu.VMEM((2, GROUPS, halves, block, ranked), HALF),
            pltpu.VMEM((2, GROUPS, 2, block, cells), SWAP),
            pltpu.VMEM((2, GROUPS, 2, block, cells), SWAP),
            pltpu.VMEM((chains, cells), FULL),
            small, small, small,
            pltpu.VMEM((halves, 8, chains), FULL),
            small, small,
            dma((6,)), dma((6,)),
            dma((2, GROUPS, halves)), dma((2, GROUPS, halves)),
            dma((2, GROUPS, 2)), dma((2, GROUPS, 2)),
            dma((2,)), dma((2,)),
            dma((halves,)), dma((halves,)),
        ],
        compiler_params=pltpu.CompilerParams(collective_id=0, has_side_effects=True),
    )(
        position, momentum,
        prepare(col_factors, col_ranks), prepare(row_factors, row_ranks),
        log_mean[None, :], counts[None, :], step_size[:, None],
    )
    return new_pos, new_mom, energy[0]


def solution(mesh):
    in_specs = (
        P(None, ("col", "row")),
        P(None, ("col", "row")),
        P(("col", "row"), None, None),
        P(("col", "row"), None, None),
        P(),
        P(("col", "row")),
        P(("col", "row")),
        P(),
    )
    out_specs = (P(None, ("col", "row")), P(None, ("col", "row")), P())
    return jax.shard_map(
        functools.partial(on_device, mesh.shape["row"]),
        mesh=mesh, in_specs=in_specs, out_specs=out_specs, check_vma=False,
    )
```

```python
import functools

import jax
import jax.numpy as jnp
from jax import lax
from jax.experimental import pallas as pl
from jax.experimental.pallas import tpu as pltpu
from jax.sharding import PartitionSpec as P

MESH = pl.DeviceIdType.MESH
GROUPS = 2
SWAP = jnp.bfloat16
FULL = jnp.float32
HALF = jnp.bfloat16
FORWARD, BACKWARD = 0, 1


def kernel(
    row_size,
    pos, mom, col_raw, row_raw, ranks, log_mean, counts, step_row,
    last_pos, mid_mom, last_force, energy, energy_rest,
    zs, ps, raw, col2, row2, col_far, row_far, lm_far, cnt_far, live, step,
    pre_out, pre_in,
    out_buf, in_buf, swap_out, swap_in, gain,
    e_own, e_far, e_chip, e_all, e_part, e_rest,
    raw_sem, init_send, init_recv, pre_send, pre_recv, send, recv, swap_send, swap_recv,
    tail_send, tail_recv, all_send, all_recv,
):
    halves = in_buf.shape[2]
    chains, cells = pos.shape
    ranked = in_buf.shape[4]
    block = chains // GROUPS

    me = lax.axis_index("col") * row_size + lax.axis_index("row")
    tile = me // 2
    core = me % 2
    side = tile % 2
    slot = tile // 2

    def address(index):
        return (index // row_size, index % row_size)

    partner = address(2 * tile + 1 - core)

    def peer(m):
        return address(2 * (2 * m + core) + side)

    def flipped(mask):
        total, bit = 0, 1
        while bit < halves:
            low = (slot // bit) % 2
            total = total + bit * ((1 - low) if mask & bit else low)
            bit *= 2
        return total

    unrolled = halves <= 8 and halves & (halves - 1) == 0
    others = [flipped(mask) for mask in range(halves - 1, 0, -1)] if unrolled else []

    def each_peer(action, at_home=None):
        if unrolled:
            for m in others:
                action(m)
        else:
            def body(n, carry):
                action((slot + 1 + n) % halves)
                return carry

            lax.fori_loop(0, halves - 1, body, 0)

        @pl.when(core != side)
        def _():
            action(slot)

        if at_home is not None:
            @pl.when(core == side)
            def _():
                at_home()

    fetch = pltpu.make_async_copy(col_raw, raw, raw_sem.at[0])
    fetch.start()
    barrier = pltpu.get_barrier_semaphore()

    def greet(m):
        pl.semaphore_signal(barrier, inc=1, device_id=peer(m), device_id_type=MESH)

    each_peer(greet)
    pl.semaphore_signal(barrier, inc=1, device_id=partner, device_id_type=MESH)
    zs[0] = pos[...]
    ps[0] = mom[...]
    gain[...] = jnp.zeros_like(gain)
    step[...] = jnp.broadcast_to(step_row[...], step.shape).T
    level = lax.broadcasted_iota(jnp.int32, (1, ranked), 1)
    for m in range(halves):
        columns = pl.ds(m * ranked, ranked)
        other = 2 * m + core
        live[FORWARD, :, columns] = (level < ranks[other, tile]).astype(FULL)
        live[BACKWARD, :, columns] = (level < ranks[tile, other]).astype(FULL)

    def rows(g):
        return pl.ds(g * block, block)

    def regroup(target):
        tiles = raw.shape[1]
        count = max(16, 1024 // tiles)

        def body(n, carry):
            some = pl.ds(pl.multiple_of(n * count, count), count)
            flat = raw[some].reshape(count, tiles * ranked)
            for parity in range(2):
                target[parity, some] = jnp.concatenate(
                    [flat[:, j * ranked:(j + 1) * ranked] for j in range(parity, tiles, 2)],
                    axis=1,
                )
            return carry

        lax.fori_loop(0, cells // count, body, 0)

    fetch.wait()
    regroup(col2)
    fetch = pltpu.make_async_copy(row_raw, raw, raw_sem.at[0])
    fetch.start()
    pl.semaphore_wait(barrier, halves + jnp.where(core == side, 0, 1))

    def remote(src, dst, s, r, where):
        return pltpu.make_async_remote_copy(
            src_ref=src, dst_ref=dst, send_sem=s, recv_sem=r,
            device_id=where, device_id_type=MESH,
        )

    def pass_on(n, src, dst):
        copy = remote(src, dst, init_send.at[n], init_recv.at[n], partner)
        copy.start()
        return copy

    def project(way, g, near, far, near_ref, far_ref):
        result = jnp.dot(near, near_ref[core], preferred_element_type=FULL)
        result += jnp.dot(far, far_ref[...], preferred_element_type=FULL)
        dispatch(way, g, result)

    def dispatch(way, g, result):
        result = (result * live[way]).astype(HALF)
        for m in range(halves):
            out_buf[way, g, m] = result[:, m * ranked:(m + 1) * ranked]

        def start(m):
            remote(
                out_buf.at[way, g, m], in_buf.at[way, g, slot],
                send.at[way, g, m], recv.at[way, g, slot], peer(m),
            ).start()

        def keep():
            in_buf[way, g, slot] = out_buf[way, g, slot]

        each_peer(start, keep)

    def expand(way, g, near_ref, far_ref):
        def finish(m):
            copy = remote(
                out_buf.at[way, g, m], in_buf.at[way, g, m],
                send.at[way, g, m], recv.at[way, g, m], peer(m),
            )
            copy.wait_recv()
            copy.wait_send()

        each_peer(finish)
        held = jnp.concatenate([in_buf[way, g, m] for m in range(halves)], axis=1)
        dims = (((1,), (1,)), ((), ()))
        copies = []
        far = lax.dot_general(held, far_ref[...], dims, preferred_element_type=FULL)
        swap_out[way, g, 1] = far.astype(SWAP)
        copies.append(remote(
            swap_out.at[way, g, 1], swap_in.at[way, g, 0],
            swap_send.at[way, g, 0], swap_recv.at[way, g, 0], partner,
        ))
        copies[0].start()
        near = lax.dot_general(held, near_ref[core], dims, preferred_element_type=FULL)
        swap_out[way, g, 0] = near.astype(SWAP)
        copies.append(remote(
            swap_out.at[way, g, 0], swap_in.at[way, g, 1],
            swap_send.at[way, g, 1], swap_recv.at[way, g, 1], partner,
        ))
        copies[1].start()
        for copy in copies:
            copy.wait()
        near = near + swap_in[way, g, 0].astype(FULL)
        far = far + swap_in[way, g, 1].astype(FULL)
        return near, far

    def send_forward(g):
        project(
            FORWARD, g,
            zs[0, rows(g)].astype(HALF), zs[1, rows(g)].astype(HALF),
            col2, col_far,
        )

    early = []
    for g in range(GROUPS):
        near = zs[0, rows(g)].astype(HALF)
        pre_out[g] = jnp.dot(near, col2[1 - core], preferred_element_type=FULL).astype(HALF)
        copy = remote(
            pre_out.at[g], pre_in.at[g], pre_send.at[g], pre_recv.at[g], partner
        )
        copy.start()
        early.append(copy)
    for g in range(GROUPS):
        near = zs[0, rows(g)].astype(HALF)
        result = jnp.dot(near, col2[core], preferred_element_type=FULL)
        early[g].wait()
        dispatch(FORWARD, g, result + pre_in[g].astype(FULL))
    later = [pass_on(0, log_mean, lm_far), pass_on(1, counts, cnt_far)]
    fetch.wait()
    regroup(row2)
    later.append(pass_on(2, row2.at[1 - core], row_far))
    later.append(pass_on(3, pos, zs.at[1]))
    later.append(pass_on(4, mom, ps.at[1]))
    later.append(pass_on(5, col2.at[1 - core], col_far))
    for copy in later:
        copy.wait()

    def section(at, carry):
        sign = (at // 2 - (2 - at) // 2).astype(FULL)
        weight = jnp.where(at == 1, 1.0, 0.5).astype(FULL)
        for g in range(GROUPS):
            near, far = expand(FORWARD, g, row2, row_far)
            exponent = log_mean[...] + near
            intensity = jnp.exp(exponent)
            rate = counts[...].astype(FULL)
            residual = (rate - intensity).astype(HALF)
            residual_far = (
                cnt_far[...].astype(FULL) - jnp.exp(lm_far[...] + far)
            ).astype(HALF)
            project(BACKWARD, g, residual, residual_far, row2, row_far)
            values = zs[0, rows(g)]
            gain[rows(g)] += sign * (
                intensity - rate * exponent + 0.5 * values * values
            )
        for g in range(GROUPS):
            pulled = expand(BACKWARD, g, col2, col_far)
            size = jnp.concatenate([step[rows(g)]] * (cells // step.shape[1]), axis=1)
            for part in range(2):
                values = zs[part, rows(g)]
                force = values - pulled[part]
                moment = ps[part, rows(g)] - weight * size * force
                ps[part, rows(g)] = moment

                if part == 0:
                    @pl.when(at == 1)
                    def _():
                        last_pos[rows(g)] = values
                        mid_mom[rows(g)] = moment

                    @pl.when(at == 2)
                    def _():
                        last_force[rows(g)] = force

                @pl.when(at < 2)
                def _():
                    zs[part, rows(g)] = values + size * moment

            @pl.when(at < 2)
            def _():
                send_forward(g)

        return carry

    lax.fori_loop(0, 3, section, 0)

    after = ps[0]
    before = mom[...]
    change = gain[...] + 0.5 * (after * after - before * before)
    lanes = e_own.shape[1]
    change = sum(change[:, n * lanes:(n + 1) * lanes] for n in range(cells // lanes))
    total = jnp.sum(change.T, axis=0, keepdims=True)
    e_own[...] = jnp.broadcast_to(total, e_own.shape)
    copy = remote(e_own, e_far, tail_send.at[0], tail_recv.at[0], partner)
    copy.start()
    copy.wait()
    e_chip[...] = e_own[...] + e_far[...]

    def spread(m):
        remote(
            e_chip, e_all.at[slot], all_send.at[m], all_recv.at[slot], peer(m)
        ).start()

    def spread_home():
        e_all[slot] = e_chip[...]

    def gather(m):
        copy = remote(e_chip, e_all.at[m], all_send.at[m], all_recv.at[m], peer(m))
        copy.wait_recv()
        copy.wait_send()

    each_peer(spread, spread_home)
    each_peer(gather)
    e_part[...] = jnp.sum(e_all[...], axis=0)
    copy = remote(e_part, e_rest, tail_send.at[1], tail_recv.at[1], partner)
    copy.start()
    copy.wait()
    energy[...] = e_part[...]
    energy_rest[...] = e_rest[...]


def on_device(
    row_size,
    position, momentum, row_factors, col_factors, tile_ranks, log_mean, counts, step_size
):
    chains, cells = position.shape
    tiles = tile_ranks.shape[0]
    halves = tiles // 2
    ranked = row_factors.shape[2]
    block = chains // GROUPS
    vmem = pl.BlockSpec(memory_space=pltpu.VMEM)
    dma = pltpu.SemaphoreType.DMA
    small = pltpu.VMEM((8, chains), FULL)
    any_space = pl.BlockSpec(memory_space=pl.ANY)
    big = jax.ShapeDtypeStruct(position.shape, FULL)
    line = jax.ShapeDtypeStruct((8, chains), FULL)
    last_pos, mid_mom, last_force, energy, energy_rest = pl.pallas_call(
        functools.partial(kernel, row_size),
        out_shape=(big, big, big, line, line),
        in_specs=[
            vmem, vmem, any_space, any_space,
            pl.BlockSpec(memory_space=pltpu.SMEM), vmem, vmem, vmem,
        ],
        out_specs=(vmem,) * 5,
        scratch_shapes=[
            pltpu.VMEM((2, chains, cells), FULL),
            pltpu.VMEM((2, chains, cells), FULL),
            pltpu.VMEM((cells, tiles, ranked), HALF),
            pltpu.VMEM((2, cells, halves * ranked), HALF),
            pltpu.VMEM((2, cells, halves * ranked), HALF),
            pltpu.VMEM((cells, halves * ranked), HALF),
            pltpu.VMEM((cells, halves * ranked), HALF),
            pltpu.VMEM((1, cells), FULL),
            pltpu.VMEM((1, cells), jnp.int32),
            pltpu.VMEM((2, 1, halves * ranked), FULL),
            pltpu.VMEM((chains, chains), FULL),
            pltpu.VMEM((GROUPS, block, halves * ranked), HALF),
            pltpu.VMEM((GROUPS, block, halves * ranked), HALF),
            pltpu.VMEM((2, GROUPS, halves, block, ranked), HALF),
            pltpu.VMEM((2, GROUPS, halves, block, ranked), HALF),
            pltpu.VMEM((2, GROUPS, 2, block, cells), SWAP),
            pltpu.VMEM((2, GROUPS, 2, block, cells), SWAP),
            pltpu.VMEM((chains, cells), FULL),
            small, small, small,
            pltpu.VMEM((halves, 8, chains), FULL),
            small, small,
            dma((1,)), dma((6,)), dma((6,)), dma((GROUPS,)), dma((GROUPS,)),
            dma((2, GROUPS, halves)), dma((2, GROUPS, halves)),
            dma((2, GROUPS, 2)), dma((2, GROUPS, 2)),
            dma((2,)), dma((2,)),
            dma((halves,)), dma((halves,)),
        ],
        compiler_params=pltpu.CompilerParams(collective_id=0, has_side_effects=True),
    )(
        position, momentum, col_factors, row_factors, tile_ranks,
        log_mean[None, :], counts[None, :], step_size[None, :],
    )
    full_step = step_size[:, None]
    new_position = last_pos + full_step * mid_mom
    new_momentum = mid_mom - 0.5 * full_step * last_force
    return new_position, new_momentum, (energy + energy_rest)[0]


def solution(mesh):
    in_specs = (
        P(None, ("col", "row")),
        P(None, ("col", "row")),
        P(("col", "row"), None, None),
        P(("col", "row"), None, None),
        P(),
        P(("col", "row")),
        P(("col", "row")),
        P(),
    )
    out_specs = (P(None, ("col", "row")), P(None, ("col", "row")), P())
    return jax.shard_map(
        functools.partial(on_device, mesh.shape["row"]),
        mesh=mesh, in_specs=in_specs, out_specs=out_specs, check_vma=False,
    )
```

```python
import functools

import jax
import jax.numpy as jnp
from jax import lax
from jax.experimental import pallas as pl
from jax.experimental.pallas import tpu as pltpu
from jax.sharding import PartitionSpec as P

MESH = pl.DeviceIdType.MESH
GROUPS = 2
SWAP = jnp.bfloat16
FULL = jnp.float32
HALF = jnp.bfloat16
FORWARD, BACKWARD = 0, 1


def kernel(
    row_size,
    pos, mom, col_raw, row_raw, ranks, log_mean, counts, step_row,
    last_pos, mid_mom, last_force, energy, energy_rest,
    zs, ps, raw, col2, row2, col_far, row_far, lm_far, cnt_far, live, step,
    pre_out, pre_in,
    out_buf, in_buf, swap_out, swap_in, gain,
    e_own, e_far, e_chip, e_all, e_part, e_rest,
    raw_sem, init_send, init_recv, pre_send, pre_recv, send, recv, swap_send, swap_recv,
    tail_send, tail_recv, all_send, all_recv,
):
    halves = in_buf.shape[2]
    chains, cells = pos.shape
    ranked = in_buf.shape[4]
    block = chains // GROUPS

    me = lax.axis_index("col") * row_size + lax.axis_index("row")
    tile = me // 2
    core = me % 2
    side = tile % 2
    slot = tile // 2

    def address(index):
        return (index // row_size, index % row_size)

    partner = address(2 * tile + 1 - core)

    def peer(m):
        return address(2 * (2 * m + core) + side)

    def flipped(mask):
        total, bit = 0, 1
        while bit < halves:
            low = (slot // bit) % 2
            total = total + bit * ((1 - low) if mask & bit else low)
            bit *= 2
        return total

    unrolled = halves <= 8 and halves & (halves - 1) == 0
    others = [flipped(mask) for mask in range(halves - 1, 0, -1)] if unrolled else []

    def each_peer(action, at_home=None):
        if unrolled:
            for m in others:
                action(m)
        else:
            def body(n, carry):
                action((slot + 1 + n) % halves)
                return carry

            lax.fori_loop(0, halves - 1, body, 0)

        @pl.when(core != side)
        def _():
            action(slot)

        if at_home is not None:
            @pl.when(core == side)
            def _():
                at_home()

    fetch = pltpu.make_async_copy(col_raw, raw, raw_sem.at[0])
    fetch.start()
    barrier = pltpu.get_barrier_semaphore()

    def greet(m):
        pl.semaphore_signal(barrier, inc=1, device_id=peer(m), device_id_type=MESH)

    each_peer(greet)
    pl.semaphore_signal(barrier, inc=1, device_id=partner, device_id_type=MESH)
    zs[0] = pos[...]
    ps[0] = mom[...]
    gain[...] = jnp.zeros_like(gain)
    step[...] = jnp.broadcast_to(step_row[...], step.shape).T
    level = lax.broadcasted_iota(jnp.int32, (1, ranked), 1)
    for m in range(halves):
        columns = pl.ds(m * ranked, ranked)
        other = 2 * m + core
        live[FORWARD, :, columns] = (level < ranks[other, tile]).astype(FULL)
        live[BACKWARD, :, columns] = (level < ranks[tile, other]).astype(FULL)

    def rows(g):
        return pl.ds(g * block, block)

    def regroup(target):
        tiles = raw.shape[1]
        count = max(16, 1024 // tiles)

        def body(n, carry):
            some = pl.ds(pl.multiple_of(n * count, count), count)
            flat = raw[some].reshape(count, tiles * ranked)
            for parity in range(2):
                target[parity, some] = jnp.concatenate(
                    [flat[:, j * ranked:(j + 1) * ranked] for j in range(parity, tiles, 2)],
                    axis=1,
                )
            return carry

        lax.fori_loop(0, cells // count, body, 0)

    fetch.wait()
    regroup(col2)
    fetch = pltpu.make_async_copy(row_raw, raw, raw_sem.at[0])
    fetch.start()
    pl.semaphore_wait(barrier, halves + jnp.where(core == side, 0, 1))

    def remote(src, dst, s, r, where):
        return pltpu.make_async_remote_copy(
            src_ref=src, dst_ref=dst, send_sem=s, recv_sem=r,
            device_id=where, device_id_type=MESH,
        )

    def pass_on(n, src, dst):
        copy = remote(src, dst, init_send.at[n], init_recv.at[n], partner)
        copy.start()
        return copy

    def project(way, g, near, far, near_ref, far_ref):
        result = jnp.dot(near, near_ref[core], preferred_element_type=FULL)
        result += jnp.dot(far(), far_ref[...], preferred_element_type=FULL)
        dispatch(way, g, result)

    def dispatch(way, g, result):
        result = (result * live[way]).astype(HALF)
        for m in range(halves):
            out_buf[way, g, m] = result[:, m * ranked:(m + 1) * ranked]

        def start(m):
            remote(
                out_buf.at[way, g, m], in_buf.at[way, g, slot],
                send.at[way, g, m], recv.at[way, g, slot], peer(m),
            ).start()

        def keep():
            in_buf[way, g, slot] = out_buf[way, g, slot]

        each_peer(start, keep)

    def expand(way, g, near_ref, far_ref):
        def finish(m):
            copy = remote(
                out_buf.at[way, g, m], in_buf.at[way, g, m],
                send.at[way, g, m], recv.at[way, g, m], peer(m),
            )
            copy.wait_recv()
            copy.wait_send()

        each_peer(finish)
        held = jnp.concatenate([in_buf[way, g, m] for m in range(halves)], axis=1)
        dims = (((1,), (1,)), ((), ()))
        copies = []
        far = lax.dot_general(held, far_ref[...], dims, preferred_element_type=FULL)
        swap_out[way, g, 1] = far.astype(SWAP)
        copies.append(remote(
            swap_out.at[way, g, 1], swap_in.at[way, g, 0],
            swap_send.at[way, g, 0], swap_recv.at[way, g, 0], partner,
        ))
        copies[0].start()
        near = lax.dot_general(held, near_ref[core], dims, preferred_element_type=FULL)
        swap_out[way, g, 0] = near.astype(SWAP)
        copies.append(remote(
            swap_out.at[way, g, 0], swap_in.at[way, g, 1],
            swap_send.at[way, g, 1], swap_recv.at[way, g, 1], partner,
        ))
        copies[1].start()
        copies[0].wait()
        near = near + swap_in[way, g, 0].astype(FULL)

        def rest():
            copies[1].wait()
            return far + swap_in[way, g, 1].astype(FULL)

        return near, rest

    def send_forward(g):
        project(
            FORWARD, g,
            zs[0, rows(g)].astype(HALF), lambda: zs[1, rows(g)].astype(HALF),
            col2, col_far,
        )

    early = []
    for g in range(GROUPS):
        near = zs[0, rows(g)].astype(HALF)
        pre_out[g] = jnp.dot(near, col2[1 - core], preferred_element_type=FULL).astype(HALF)
        copy = remote(
            pre_out.at[g], pre_in.at[g], pre_send.at[g], pre_recv.at[g], partner
        )
        copy.start()
        early.append(copy)
    for g in range(GROUPS):
        near = zs[0, rows(g)].astype(HALF)
        result = jnp.dot(near, col2[core], preferred_element_type=FULL)
        early[g].wait()
        dispatch(FORWARD, g, result + pre_in[g].astype(FULL))
    later = [pass_on(0, log_mean, lm_far), pass_on(1, counts, cnt_far)]
    fetch.wait()
    regroup(row2)
    later.append(pass_on(2, row2.at[1 - core], row_far))
    later.append(pass_on(3, pos, zs.at[1]))
    later.append(pass_on(4, mom, ps.at[1]))
    later.append(pass_on(5, col2.at[1 - core], col_far))
    for copy in later:
        copy.wait()

    def section(at, carry):
        sign = (at // 2 - (2 - at) // 2).astype(FULL)
        weight = jnp.where(at == 1, 1.0, 0.5).astype(FULL)
        for g in range(GROUPS):
            near, far = expand(FORWARD, g, row2, row_far)
            exponent = log_mean[...] + near
            intensity = jnp.exp(exponent)
            rate = counts[...].astype(FULL)
            residual = (rate - intensity).astype(HALF)

            def residual_far():
                intensity_far = jnp.exp(lm_far[...] + far())
                return (cnt_far[...].astype(FULL) - intensity_far).astype(HALF)

            project(BACKWARD, g, residual, residual_far, row2, row_far)
            values = zs[0, rows(g)]
            gain[rows(g)] += sign * (
                intensity - rate * exponent + 0.5 * values * values
            )
        for g in range(GROUPS):
            pulled = expand(BACKWARD, g, col2, col_far)
            size = jnp.concatenate([step[rows(g)]] * (cells // step.shape[1]), axis=1)
            for part in range(2):
                values = zs[part, rows(g)]
                force = values - (pulled[0] if part == 0 else pulled[1]())
                moment = ps[part, rows(g)] - weight * size * force
                ps[part, rows(g)] = moment

                if part == 0:
                    @pl.when(at == 1)
                    def _():
                        last_pos[rows(g)] = values
                        mid_mom[rows(g)] = moment

                    @pl.when(at == 2)
                    def _():
                        last_force[rows(g)] = force

                @pl.when(at < 2)
                def _():
                    zs[part, rows(g)] = values + size * moment

            @pl.when(at < 2)
            def _():
                send_forward(g)

        return carry

    lax.fori_loop(0, 3, section, 0)

    after = ps[0]
    before = mom[...]
    change = gain[...] + 0.5 * (after * after - before * before)
    lanes = e_own.shape[1]
    change = sum(change[:, n * lanes:(n + 1) * lanes] for n in range(cells // lanes))
    total = jnp.sum(change.T, axis=0, keepdims=True)
    e_own[...] = jnp.broadcast_to(total, e_own.shape)
    copy = remote(e_own, e_far, tail_send.at[0], tail_recv.at[0], partner)
    copy.start()
    copy.wait()
    e_chip[...] = e_own[...] + e_far[...]

    def spread(m):
        remote(
            e_chip, e_all.at[slot], all_send.at[m], all_recv.at[slot], peer(m)
        ).start()

    def spread_home():
        e_all[slot] = e_chip[...]

    def gather(m):
        copy = remote(e_chip, e_all.at[m], all_send.at[m], all_recv.at[m], peer(m))
        copy.wait_recv()
        copy.wait_send()

    each_peer(spread, spread_home)
    each_peer(gather)
    e_part[...] = jnp.sum(e_all[...], axis=0)
    copy = remote(e_part, e_rest, tail_send.at[1], tail_recv.at[1], partner)
    copy.start()
    copy.wait()
    energy[...] = e_part[...]
    energy_rest[...] = e_rest[...]


def on_device(
    row_size,
    position, momentum, row_factors, col_factors, tile_ranks, log_mean, counts, step_size
):
    chains, cells = position.shape
    tiles = tile_ranks.shape[0]
    halves = tiles // 2
    ranked = row_factors.shape[2]
    block = chains // GROUPS
    vmem = pl.BlockSpec(memory_space=pltpu.VMEM)
    dma = pltpu.SemaphoreType.DMA
    small = pltpu.VMEM((8, chains), FULL)
    any_space = pl.BlockSpec(memory_space=pl.ANY)
    big = jax.ShapeDtypeStruct(position.shape, FULL)
    line = jax.ShapeDtypeStruct((8, chains), FULL)
    last_pos, mid_mom, last_force, energy, energy_rest = pl.pallas_call(
        functools.partial(kernel, row_size),
        out_shape=(big, big, big, line, line),
        in_specs=[
            vmem, vmem, any_space, any_space,
            pl.BlockSpec(memory_space=pltpu.SMEM), vmem, vmem, vmem,
        ],
        out_specs=(vmem,) * 5,
        scratch_shapes=[
            pltpu.VMEM((2, chains, cells), FULL),
            pltpu.VMEM((2, chains, cells), FULL),
            pltpu.VMEM((cells, tiles, ranked), HALF),
            pltpu.VMEM((2, cells, halves * ranked), HALF),
            pltpu.VMEM((2, cells, halves * ranked), HALF),
            pltpu.VMEM((cells, halves * ranked), HALF),
            pltpu.VMEM((cells, halves * ranked), HALF),
            pltpu.VMEM((1, cells), FULL),
            pltpu.VMEM((1, cells), jnp.int32),
            pltpu.VMEM((2, 1, halves * ranked), FULL),
            pltpu.VMEM((chains, chains), FULL),
            pltpu.VMEM((GROUPS, block, halves * ranked), HALF),
            pltpu.VMEM((GROUPS, block, halves * ranked), HALF),
            pltpu.VMEM((2, GROUPS, halves, block, ranked), HALF),
            pltpu.VMEM((2, GROUPS, halves, block, ranked), HALF),
            pltpu.VMEM((2, GROUPS, 2, block, cells), SWAP),
            pltpu.VMEM((2, GROUPS, 2, block, cells), SWAP),
            pltpu.VMEM((chains, cells), FULL),
            small, small, small,
            pltpu.VMEM((halves, 8, chains), FULL),
            small, small,
            dma((1,)), dma((6,)), dma((6,)), dma((GROUPS,)), dma((GROUPS,)),
            dma((2, GROUPS, halves)), dma((2, GROUPS, halves)),
            dma((2, GROUPS, 2)), dma((2, GROUPS, 2)),
            dma((2,)), dma((2,)),
            dma((halves,)), dma((halves,)),
        ],
        compiler_params=pltpu.CompilerParams(collective_id=0, has_side_effects=True),
    )(
        position, momentum, col_factors, row_factors, tile_ranks,
        log_mean[None, :], counts[None, :], step_size[None, :],
    )
    full_step = step_size[:, None]
    new_position = last_pos + full_step * mid_mom
    new_momentum = mid_mom - full_step * (0.5 * last_force)
    return new_position, new_momentum, energy[0] + energy_rest[0]


def solution(mesh):
    in_specs = (
        P(None, ("col", "row")),
        P(None, ("col", "row")),
        P(("col", "row"), None, None),
        P(("col", "row"), None, None),
        P(),
        P(("col", "row")),
        P(("col", "row")),
        P(),
    )
    out_specs = (P(None, ("col", "row")), P(None, ("col", "row")), P())
    return jax.shard_map(
        functools.partial(on_device, mesh.shape["row"]),
        mesh=mesh, in_specs=in_specs, out_specs=out_specs, check_vma=False,
    )
```

```python
import functools

import jax
import jax.numpy as jnp
from jax import lax
from jax.experimental import pallas as pl
from jax.experimental.pallas import tpu as pltpu
from jax.sharding import PartitionSpec as P

MESH = pl.DeviceIdType.MESH
GROUPS = 2
SWAP = jnp.bfloat16
FULL = jnp.float32
HALF = jnp.bfloat16
FORWARD, BACKWARD = 0, 1


def kernel(
    row_size,
    pos, mom, col_raw, row_raw, ranks, log_mean, counts, step_row,
    last_pos, mid_mom, last_force, energy, energy_rest,
    zs, ps, raw, col2, row2, col_far, row_far, lm_far, cnt_far, live, step,
    pre_out, pre_in,
    out_buf, in_buf, swap_out, swap_in, gain,
    e_own, e_far, e_chip, e_all, e_part, e_rest,
    raw_sem, init_send, init_recv, pre_send, pre_recv, send, recv, swap_send, swap_recv,
    tail_send, tail_recv, all_send, all_recv,
):
    halves = in_buf.shape[2]
    chains, cells = pos.shape
    ranked = in_buf.shape[4]
    block = chains // GROUPS

    me = lax.axis_index("col") * row_size + lax.axis_index("row")
    tile = me // 2
    core = me % 2
    side = tile % 2
    slot = tile // 2

    def address(index):
        return (index // row_size, index % row_size)

    partner = address(2 * tile + 1 - core)

    def peer(m):
        return address(2 * (2 * m + core) + side)

    def flipped(mask):
        total, bit = 0, 1
        while bit < halves:
            low = (slot // bit) % 2
            total = total + bit * ((1 - low) if mask & bit else low)
            bit *= 2
        return total

    unrolled = halves <= 8 and halves & (halves - 1) == 0
    others = [flipped(mask) for mask in range(halves - 1, 0, -1)] if unrolled else []

    def each_peer(action, at_home=None):
        if unrolled:
            for m in others:
                action(m)
        else:
            def body(n, carry):
                action((slot + 1 + n) % halves)
                return carry

            lax.fori_loop(0, halves - 1, body, 0)

        @pl.when(core != side)
        def _():
            action(slot)

        if at_home is not None:
            @pl.when(core == side)
            def _():
                at_home()

    fetch = pltpu.make_async_copy(col_raw, raw, raw_sem.at[0])
    fetch.start()
    barrier = pltpu.get_barrier_semaphore()

    def greet(m):
        pl.semaphore_signal(barrier, inc=1, device_id=peer(m), device_id_type=MESH)

    each_peer(greet)
    pl.semaphore_signal(barrier, inc=1, device_id=partner, device_id_type=MESH)
    zs[0] = pos[...]
    ps[0] = mom[...]
    gain[...] = jnp.zeros_like(gain)
    step[...] = jnp.broadcast_to(step_row[...], step.shape).T
    level = lax.broadcasted_iota(jnp.int32, (1, ranked), 1)
    for m in range(halves):
        columns = pl.ds(m * ranked, ranked)
        other = 2 * m + core
        live[FORWARD, :, columns] = (level < ranks[other, tile]).astype(FULL)
        live[BACKWARD, :, columns] = (level < ranks[tile, other]).astype(FULL)

    def rows(g):
        return pl.ds(g * block, block)

    def regroup(target):
        tiles = raw.shape[1]
        count = max(16, 1024 // tiles)

        def body(n, carry):
            some = pl.ds(pl.multiple_of(n * count, count), count)
            flat = raw[some].reshape(count, tiles * ranked)
            for parity in range(2):
                target[parity, some] = jnp.concatenate(
                    [flat[:, j * ranked:(j + 1) * ranked] for j in range(parity, tiles, 2)],
                    axis=1,
                )
            return carry

        lax.fori_loop(0, cells // count, body, 0)

    fetch.wait()
    regroup(col2)
    fetch = pltpu.make_async_copy(row_raw, raw, raw_sem.at[0])
    fetch.start()
    pl.semaphore_wait(barrier, halves + jnp.where(core == side, 0, 1))

    def remote(src, dst, s, r, where):
        return pltpu.make_async_remote_copy(
            src_ref=src, dst_ref=dst, send_sem=s, recv_sem=r,
            device_id=where, device_id_type=MESH,
        )

    def pass_on(n, src, dst):
        copy = remote(src, dst, init_send.at[n], init_recv.at[n], partner)
        copy.start()
        return copy

    def project(way, g, near, far, near_ref, far_ref):
        result = jnp.dot(near, near_ref[core], preferred_element_type=FULL)
        result += jnp.dot(far(), far_ref[...], preferred_element_type=FULL)
        dispatch(way, g, result)

    def dispatch(way, g, result):
        result = (result * live[way]).astype(HALF)
        for m in range(halves):
            out_buf[way, g, m] = result[:, m * ranked:(m + 1) * ranked]

        def start(m):
            remote(
                out_buf.at[way, g, m], in_buf.at[way, g, slot],
                send.at[way, g, m], recv.at[way, g, slot], peer(m),
            ).start()

        def keep():
            in_buf[way, g, slot] = out_buf[way, g, slot]

        each_peer(start, keep)

    def expand(way, g, near_ref, far_ref):
        def finish(m):
            copy = remote(
                out_buf.at[way, g, m], in_buf.at[way, g, m],
                send.at[way, g, m], recv.at[way, g, m], peer(m),
            )
            copy.wait_recv()

        def release(m):
            remote(
                out_buf.at[way, g, m], in_buf.at[way, g, m],
                send.at[way, g, m], recv.at[way, g, m], peer(m),
            ).wait_send()

        each_peer(finish)
        held = jnp.concatenate([in_buf[way, g, m] for m in range(halves)], axis=1)
        dims = (((1,), (1,)), ((), ()))
        copies = []
        far = lax.dot_general(held, far_ref[...], dims, preferred_element_type=FULL)
        swap_out[way, g, 1] = far.astype(SWAP)
        copies.append(remote(
            swap_out.at[way, g, 1], swap_in.at[way, g, 0],
            swap_send.at[way, g, 0], swap_recv.at[way, g, 0], partner,
        ))
        copies[0].start()
        near = lax.dot_general(held, near_ref[core], dims, preferred_element_type=FULL)
        swap_out[way, g, 0] = near.astype(SWAP)
        copies.append(remote(
            swap_out.at[way, g, 0], swap_in.at[way, g, 1],
            swap_send.at[way, g, 1], swap_recv.at[way, g, 1], partner,
        ))
        copies[1].start()
        each_peer(release)
        copies[0].wait()
        near = near + swap_in[way, g, 0].astype(FULL)

        def rest():
            copies[1].wait()
            return far + swap_in[way, g, 1].astype(FULL)

        return near, rest

    def send_forward(g):
        project(
            FORWARD, g,
            zs[0, rows(g)].astype(HALF), lambda: zs[1, rows(g)].astype(HALF),
            col2, col_far,
        )

    early = []
    for g in range(GROUPS):
        near = zs[0, rows(g)].astype(HALF)
        pre_out[g] = jnp.dot(near, col2[1 - core], preferred_element_type=FULL).astype(HALF)
        copy = remote(
            pre_out.at[g], pre_in.at[g], pre_send.at[g], pre_recv.at[g], partner
        )
        copy.start()
        early.append(copy)
    for g in range(GROUPS):
        near = zs[0, rows(g)].astype(HALF)
        result = jnp.dot(near, col2[core], preferred_element_type=FULL)
        early[g].wait()
        dispatch(FORWARD, g, result + pre_in[g].astype(FULL))
    later = [pass_on(0, log_mean, lm_far), pass_on(1, counts, cnt_far)]
    fetch.wait()
    regroup(row2)
    later.append(pass_on(2, row2.at[1 - core], row_far))
    later.append(pass_on(3, pos, zs.at[1]))
    later.append(pass_on(4, mom, ps.at[1]))
    later.append(pass_on(5, col2.at[1 - core], col_far))
    for copy in later:
        copy.wait()

    def section(at, carry):
        sign = (at // 2 - (2 - at) // 2).astype(FULL)
        weight = jnp.where(at == 1, 1.0, 0.5).astype(FULL)
        for g in range(GROUPS):
            near, far = expand(FORWARD, g, row2, row_far)
            exponent = log_mean[...] + near
            intensity = jnp.exp(exponent)
            rate = counts[...].astype(FULL)
            residual = (rate - intensity).astype(HALF)

            def residual_far():
                intensity_far = jnp.exp(lm_far[...] + far())
                return (cnt_far[...].astype(FULL) - intensity_far).astype(HALF)

            project(BACKWARD, g, residual, residual_far, row2, row_far)
            values = zs[0, rows(g)]
            gain[rows(g)] += sign * (
                intensity - rate * exponent + 0.5 * values * values
            )
        for g in range(GROUPS):
            pulled = expand(BACKWARD, g, col2, col_far)
            size = jnp.concatenate([step[rows(g)]] * (cells // step.shape[1]), axis=1)
            for part in range(2):
                values = zs[part, rows(g)]
                force = values - (pulled[0] if part == 0 else pulled[1]())
                moment = ps[part, rows(g)] - weight * size * force
                ps[part, rows(g)] = moment

                if part == 0:
                    @pl.when(at == 1)
                    def _():
                        last_pos[rows(g)] = values
                        mid_mom[rows(g)] = moment

                    @pl.when(at == 2)
                    def _():
                        last_force[rows(g)] = force

                @pl.when(at < 2)
                def _():
                    zs[part, rows(g)] = values + size * moment

            @pl.when(at < 2)
            def _():
                send_forward(g)

        return carry

    lax.fori_loop(0, 3, section, 0)

    after = ps[0]
    before = mom[...]
    change = gain[...] + 0.5 * (after * after - before * before)
    lanes = e_own.shape[1]
    change = sum(change[:, n * lanes:(n + 1) * lanes] for n in range(cells // lanes))
    total = jnp.sum(change.T, axis=0, keepdims=True)
    e_own[...] = jnp.broadcast_to(total, e_own.shape)
    copy = remote(e_own, e_far, tail_send.at[0], tail_recv.at[0], partner)
    copy.start()
    copy.wait()
    e_chip[...] = e_own[...] + e_far[...]

    def spread(m):
        remote(
            e_chip, e_all.at[slot], all_send.at[m], all_recv.at[slot], peer(m)
        ).start()

    def spread_home():
        e_all[slot] = e_chip[...]

    def gather(m):
        copy = remote(e_chip, e_all.at[m], all_send.at[m], all_recv.at[m], peer(m))
        copy.wait_recv()
        copy.wait_send()

    each_peer(spread, spread_home)
    each_peer(gather)
    e_part[...] = jnp.sum(e_all[...], axis=0)
    copy = remote(e_part, e_rest, tail_send.at[1], tail_recv.at[1], partner)
    copy.start()
    copy.wait()
    energy[...] = e_part[...]
    energy_rest[...] = e_rest[...]


def on_device(
    row_size,
    position, momentum, row_factors, col_factors, tile_ranks, log_mean, counts, step_size
):
    chains, cells = position.shape
    tiles = tile_ranks.shape[0]
    halves = tiles // 2
    ranked = row_factors.shape[2]
    block = chains // GROUPS
    vmem = pl.BlockSpec(memory_space=pltpu.VMEM)
    dma = pltpu.SemaphoreType.DMA
    small = pltpu.VMEM((8, chains), FULL)
    any_space = pl.BlockSpec(memory_space=pl.ANY)
    big = jax.ShapeDtypeStruct(position.shape, FULL)
    line = jax.ShapeDtypeStruct((8, chains), FULL)
    last_pos, mid_mom, last_force, energy, energy_rest = pl.pallas_call(
        functools.partial(kernel, row_size),
        out_shape=(big, big, big, line, line),
        in_specs=[
            vmem, vmem, any_space, any_space,
            pl.BlockSpec(memory_space=pltpu.SMEM), vmem, vmem, vmem,
        ],
        out_specs=(vmem,) * 5,
        scratch_shapes=[
            pltpu.VMEM((2, chains, cells), FULL),
            pltpu.VMEM((2, chains, cells), FULL),
            pltpu.VMEM((cells, tiles, ranked), HALF),
            pltpu.VMEM((2, cells, halves * ranked), HALF),
            pltpu.VMEM((2, cells, halves * ranked), HALF),
            pltpu.VMEM((cells, halves * ranked), HALF),
            pltpu.VMEM((cells, halves * ranked), HALF),
            pltpu.VMEM((1, cells), FULL),
            pltpu.VMEM((1, cells), jnp.int32),
            pltpu.VMEM((2, 1, halves * ranked), FULL),
            pltpu.VMEM((chains, chains), FULL),
            pltpu.VMEM((GROUPS, block, halves * ranked), HALF),
            pltpu.VMEM((GROUPS, block, halves * ranked), HALF),
            pltpu.VMEM((2, GROUPS, halves, block, ranked), HALF),
            pltpu.VMEM((2, GROUPS, halves, block, ranked), HALF),
            pltpu.VMEM((2, GROUPS, 2, block, cells), SWAP),
            pltpu.VMEM((2, GROUPS, 2, block, cells), SWAP),
            pltpu.VMEM((chains, cells), FULL),
            small, small, small,
            pltpu.VMEM((halves, 8, chains), FULL),
            small, small,
            dma((1,)), dma((6,)), dma((6,)), dma((GROUPS,)), dma((GROUPS,)),
            dma((2, GROUPS, halves)), dma((2, GROUPS, halves)),
            dma((2, GROUPS, 2)), dma((2, GROUPS, 2)),
            dma((2,)), dma((2,)),
            dma((halves,)), dma((halves,)),
        ],
        compiler_params=pltpu.CompilerParams(collective_id=0, has_side_effects=True),
    )(
        position, momentum, col_factors, row_factors, tile_ranks,
        log_mean[None, :], counts[None, :], step_size[None, :],
    )
    full_step = step_size[:, None]
    new_position = last_pos + full_step * mid_mom
    new_momentum = mid_mom - full_step * (0.5 * last_force)
    return new_position, new_momentum, energy[0] + energy_rest[0]


def solution(mesh):
    in_specs = (
        P(None, ("col", "row")),
        P(None, ("col", "row")),
        P(("col", "row"), None, None),
        P(("col", "row"), None, None),
        P(),
        P(("col", "row")),
        P(("col", "row")),
        P(),
    )
    out_specs = (P(None, ("col", "row")), P(None, ("col", "row")), P())
    return jax.shard_map(
        functools.partial(on_device, mesh.shape["row"]),
        mesh=mesh, in_specs=in_specs, out_specs=out_specs, check_vma=False,
    )
```
